32 devices in a mesh: orb: 8 (over z, y), fit: 4 (over x, core).
Axes of the slice: x: 2, y: 2, z: 4, core: 2. Of those that a mesh axis runs over, the one named last changes fastest.
Arguments:
- fit_ints: bfloat16 [8, 4096, 512], P('orb', 'fit'), may hold values from -0.75 to 0.75
- virt_fock: bfloat16 [8, 512, 512], P('orb'), may hold values from -1 to 3, as said below
- occ_energy: float32 [8], replicated, may hold values from -2 to -0.3
- partner: int32 [16], P('orb'), may hold values from 0 to 7, as said below
- old_amps: bfloat16 [16, 512, 512], P('orb'), may hold values from -2 to 2
Outputs:
- new_amps: bfloat16 [16, 512, 512], P('orb')
- density_grad: bfloat16 [8, 4096, 512], P('orb', 'fit')
The draws below stay inside these ranges and needn't reach their ends.
Inputs may be any that keep to these rules, and one draw needn't show every extreme that they name: partner[p] lies within 2 of orbital p // 2; the first pair of every orbital is at distance exactly 2. `virt_fock`: each block is symmetric, with diagonal entries from 0.5 to 3.
All inputs are finite; a program needn't handle non-finite values.
Results may differ from the reference program's by a relative error of at most 0.0045.
Values may be sent and summed in bfloat16 or wider, within the bound.
No kernel may reach another device: no remote copies, remote signals or barrier semaphores. Data moves between devices by JAX's collectives and lax.ppermute only.
A program may use at most 64 MiB of HBM per device.

```python
import jax
import jax.numpy as jnp
from jax import lax

NV = 512
NFIT = 4096
PAIR_DEV = 2
REACH = 2
NORB = 8
NPAIR = 16


def draw_partner(key, part):
    ids = jnp.arange(NPAIR).astype(jnp.int32)
    owner = ids // PAIR_DEV
    first = ids % PAIR_DEV == 0
    lowest = jnp.maximum(-REACH, -owner)
    highest = jnp.minimum(REACH, NORB - 1 - owner)
    key_a, key_b = jax.random.split(key)
    raw_bits = jax.random.randint(key_a, (NPAIR,), 0, 1 << 20)
    spread = lowest + raw_bits % (highest - lowest + 1)
    coin = jax.random.randint(key_b, (NPAIR,), 0, 2)
    edge = jnp.where(coin == 1, REACH, -REACH)
    edge = jnp.where(owner - REACH < 0, REACH, edge)
    edge = jnp.where(owner + REACH > NORB - 1, -REACH, edge)
    return (owner + jnp.where(first, edge, spread)).astype(jnp.int32)


def draw_virt_fock(key, part):
    key_a, key_b = jax.random.split(key)
    diagonal = jax.random.uniform(key_a, (NORB, NV), jnp.float32, 0.5, 3.0)
    offdiag = 0.04 * jax.random.normal(key_b, (NORB, NV, NV), jnp.float32)
    symmetric = (offdiag + jnp.swapaxes(offdiag, 1, 2)) * 0.7071
    identity = jnp.eye(NV, dtype=jnp.float32)
    return (symmetric * (1.0 - identity) + diagonal[:, :, None] * identity).astype(jnp.bfloat16)


def levels(stream_key, shape, cuts, least, largest):
    def one(position, parts):
        heights = jax.random.uniform(jax.random.fold_in(jax.random.fold_in(stream_key, 6), position), (parts,), jnp.float32, least / len(cuts), largest / len(cuts))
        return jnp.repeat(jnp.exp(heights), shape[position] // parts).reshape((-1,) + (1,) * (len(shape) - position - 1))

    loudness = one(*cuts[0])
    for cut in cuts[1:]:
        loudness = loudness * one(*cut)
    return loudness


def scatter_about(stream_key, shape, deviation, bound, shards=(), held_as=jnp.bfloat16):
    values = jax.random.normal(stream_key, shape, jnp.float32) * deviation
    if len(shards) > 0:
        values = levels(stream_key, shape, shards, -0.22, 0.18) * values
    return jnp.clip(values, min=-bound, max=bound).astype(held_as)


def setup_inputs(seed: int = 0) -> dict:
    splits = jax.random.split(jax.random.key(seed), 6)
    return {
        "fit_ints": scatter_about(splits[0], (NORB, NFIT, NV), (NFIT // 64) ** -0.5, 0.75, ((0, 8), (1, 4))),
        "virt_fock": draw_virt_fock(jax.random.fold_in(splits[5], 71), 0),
        "occ_energy": jnp.clip(jax.random.uniform(splits[2], (NORB,), jnp.float32, -2.0, -0.3), -2.0, -0.3),
        "partner": draw_partner(jax.random.fold_in(splits[5], 71), 0),
        "old_amps": scatter_about(splits[4], (NPAIR, NV, NV), 0.3, 2.0, ((0, 8),)),
    }


def reference(fit_ints, virt_fock, occ_energy, partner, old_amps):
    offsets = jnp.arange(-REACH, REACH + 1).astype(jnp.int32)

    def orbital(grad_sum, index):
        ints_i = fit_ints[index]
        fock_i = virt_fock[index]
        diag_i = jnp.diagonal(fock_i).astype(jnp.float32)
        partners = lax.dynamic_slice_in_dim(partner, index * PAIR_DEV, PAIR_DEV)
        amps_block = lax.dynamic_slice_in_dim(old_amps, index * PAIR_DEV, PAIR_DEV, 0)
        own_term = jnp.zeros((NFIT, NV), jnp.float32)
        results = []
        for pair_slot in range(PAIR_DEV):
            index_j = partners[pair_slot]
            ints_j = fit_ints[index_j]
            fock_j = virt_fock[index_j]
            amps = amps_block[pair_slot]
            coulomb = lax.dot_general(ints_i, ints_j, (((0,), (0,)), ((), ())), preferred_element_type=jnp.float32)
            shift_sum = occ_energy[index] + occ_energy[index_j]
            residual = coulomb + jnp.dot(fock_i, amps, preferred_element_type=jnp.float32)
            residual = residual + jnp.dot(amps, fock_j, preferred_element_type=jnp.float32)
            residual = residual - shift_sum * amps.astype(jnp.float32)
            denominator = diag_i[:, None] + jnp.diagonal(fock_j).astype(jnp.float32)[None, :] - shift_sum
            amps_new = (amps.astype(jnp.float32) - residual / denominator).astype(jnp.bfloat16)
            own_term = own_term + lax.dot_general(ints_j, amps_new, (((1,), (1,)), ((), ())), preferred_element_type=jnp.float32)
            results.append(amps_new)
        weights = (partners[:, None] - index == offsets[None, :]).astype(jnp.float32)
        amp_sums = jnp.einsum("po,pab->oab", weights, jnp.stack(results).astype(jnp.float32)).astype(jnp.bfloat16)
        center = jnp.dot(ints_i, amp_sums[REACH], preferred_element_type=jnp.float32)
        grad_sum = grad_sum.at[index].add(own_term + center)
        for shift_step in range(-REACH, REACH + 1):
            if shift_step != 0:
                product = jnp.dot(ints_i, amp_sums[shift_step + REACH], preferred_element_type=jnp.float32)
                outgoing = lax.optimization_barrier(product.astype(jnp.bfloat16))
                target = jnp.clip(index + shift_step, 0, NORB - 1)
                grad_sum = grad_sum.at[target].add(outgoing.astype(jnp.float32))
        return grad_sum, jnp.stack(results)

    start_sum = jnp.zeros((NORB, NFIT, NV), jnp.float32)
    grad_sum, amps_all = lax.scan(orbital, start_sum, jnp.arange(NORB).astype(jnp.int32))
    return amps_all.reshape(NPAIR, NV, NV), grad_sum.astype(jnp.bfloat16)
```

```python
import functools

import jax
import jax.numpy as jnp
from jax import lax
from jax.experimental import pallas as pl
from jax.experimental.pallas import tpu as pltpu
from jax.sharding import PartitionSpec as P

REACH = 2
F32 = jnp.float32
BF16 = jnp.bfloat16
WIRE = jnp.float16
COUNT_ROWS = 16

SMEM = pl.BlockSpec(memory_space=pltpu.SMEM)
VMEM = pl.BlockSpec(memory_space=pltpu.VMEM)

NN = (((1,), (0,)), ((), ()))
NT = (((1,), (1,)), ((), ()))
TN = (((0,), (0,)), ((), ()))


def mm(a, b, dims):
    return lax.dot_general(a, b, dims, preferred_element_type=F32)


def kernel_call(body, outs, scalars, arrays, name, scratch=()):
    single = not isinstance(outs, (list, tuple))
    return pl.pallas_call(
        body,
        out_shape=outs,
        in_specs=[SMEM] * len(scalars) + [VMEM] * len(arrays),
        out_specs=VMEM if single else [VMEM] * len(outs),
        scratch_shapes=scratch,
        name=name,
    )(*scalars, *arrays)


def offsets_of(orb):
    to_y = 1 - 2 * (orb % 2)
    return (REACH, -REACH, to_y, -to_y)


def slab_ds(fit, width):
    return pl.ds(pl.multiple_of(fit * width, width), width)


def side_body(fit_ref, orb_ref, partner_ref, fock_ref, amps_ref, *outs):
    width = (outs[0].shape[0] - COUNT_ROWS) // 3
    rows = slab_ds(fit_ref[0], width)
    fock_rows = fock_ref[rows, :]
    orb = orb_ref[0]
    pairs = amps_ref.shape[0]
    amp_rows = [amps_ref[p, rows, :].astype(F32) for p in range(pairs)]
    prods = [mm(fock_rows, amps_ref[p], NN) for p in range(pairs)]
    for out, offset in zip(outs, offsets_of(orb)):
        amp_sum = jnp.zeros_like(amp_rows[0])
        prod_sum = jnp.zeros_like(amp_rows[0])
        count = jnp.float32(0)
        for p in range(pairs):
            hit = (partner_ref[p] - orb == offset).astype(F32)
            amp_sum = amp_sum + hit * amp_rows[p]
            prod_sum = prod_sum + hit * prods[p]
            count = count + hit
        out[:width, :] = amp_sum.astype(BF16)
        out[width : 2 * width, :] = prod_sum.astype(BF16)
        out[2 * width : 3 * width, :] = fock_rows
        out[3 * width :, :] = jnp.full((COUNT_ROWS, fock_rows.shape[1]), count, F32).astype(BF16)


def blocks_body(fit_ref, own_ref, *refs):
    count = (len(refs) - 2)
    near, keep, send = refs[:count], refs[count], refs[count + 1]
    fits = 2 * keep.shape[1]
    width = keep.shape[2]
    fit = fit_ref[0]
    own = own_ref[...]
    for n, ref in enumerate(near):
        prod = mm(ref[...], own, TN)
        for s in range(fits):
            place = s ^ fit
            tile = prod[s * width : (s + 1) * width]

            @pl.when(place % 2 == 0)
            def _():
                keep[n, place // 2] = tile

            @pl.when(place % 2 == 1)
            def _():
                send[n, place // 2] = tile


def split_body(fit_ref, own_ref, low_ref, high_ref, keep, send):
    fits = 2 * keep.shape[1]
    width = keep.shape[2]
    half = low_ref.shape[0]
    fit = fit_ref[0]
    prod = mm(low_ref[...], own_ref[:half], TN) + mm(high_ref[...], own_ref[half:], TN)
    for s in range(fits):
        place = s ^ fit
        tile = prod[s * width : (s + 1) * width]

        @pl.when(place % 2 == 0)
        def _():
            keep[0, place // 2] = tile

        @pl.when(place % 2 == 1)
        def _():
            send[0, place // 2] = tile


def diag_row(fock):
    size = fock.shape[0]
    eye = lax.broadcasted_iota(jnp.int32, (size, size), 0) == lax.broadcasted_iota(
        jnp.int32, (size, size), 1
    )
    return jnp.sum(jnp.where(eye, fock.astype(F32), 0.0), axis=0, keepdims=True)


def diag_col(fock_rows_ref, start, fit, width):
    block = fock_rows_ref[start : start + width, slab_ds(fit, width)].astype(F32)
    eye = lax.broadcasted_iota(jnp.int32, (width, width), 0) == lax.broadcasted_iota(
        jnp.int32, (width, width), 1
    )
    return jnp.sum(jnp.where(eye, block, 0.0), axis=1, keepdims=True)


def energy_sum(energy_ref, orb, other):
    top = energy_ref.shape[0] - 1
    return energy_ref[orb] + energy_ref[jnp.clip(other, 0, top)]


def incoming(block, side_ref, fit, fock, drow, shift):
    width = block.shape[0]
    amps = side_ref[:width, :]
    wide = amps.astype(F32)
    count = side_ref[3 * width : 3 * width + 1, :].astype(F32)
    residual = count * block + side_ref[width : 2 * width, :].astype(F32)
    residual = residual + mm(amps, fock, NN) - shift * wide
    denominator = diag_col(side_ref, 2 * width, fit, width) + drow - shift
    return (wide - residual / denominator).astype(BF16)


def own_pair(block, fock_rows, dcol, amps_ref, p, fit, fock, drow, shift):
    width = block.shape[0]
    turned = amps_ref[p, :, slab_ds(fit, width)].astype(F32).T
    residual = block + mm(turned.astype(BF16), fock, NN) + mm(fock_rows, amps_ref[p], NT)
    residual = residual - shift * turned
    return (turned - residual / (dcol + drow - shift)).astype(BF16)


def early_body(
    fit_ref, orb_ref, partner_ref, energy_ref, block_ref, up_ref, down_ref, y_ref, fock_ref, amps_ref, out
):
    fit = fit_ref[0]
    orb = orb_ref[0]
    fock = fock_ref[...]
    drow = diag_row(fock)
    width = out.shape[1]
    sides = (up_ref, down_ref, y_ref)
    for n, offset in enumerate(offsets_of(orb)[:3]):
        shift = energy_sum(energy_ref, orb, orb + offset)
        out[1 + n] = incoming(block_ref[n], sides[n], fit, fock, drow, shift)
    for n, offset in enumerate((REACH, -REACH)):

        @pl.when(partner_ref[0] - orb == offset)
        def _():
            side = sides[n]
            out[0] = own_pair(
                block_ref[n],
                side[2 * width : 3 * width, :],
                diag_col(side, 2 * width, fit, width),
                amps_ref,
                0,
                fit,
                fock,
                drow,
                energy_sum(energy_ref, orb, orb + offset),
            )


def late_body(
    fit_ref,
    orb_ref,
    partner_ref,
    energy_ref,
    block_ref,
    self_ref,
    cross_ref,
    up_ref,
    down_ref,
    y_ref,
    c_ref,
    fock_ref,
    amps_ref,
    out,
):
    fit = fit_ref[0]
    orb = orb_ref[0]
    fock = fock_ref[...]
    drow = diag_row(fock)
    width = out.shape[1]
    sides = (up_ref, down_ref, y_ref, c_ref)
    offsets = offsets_of(orb)
    shift = energy_sum(energy_ref, orb, orb + offsets[3])
    pairs = amps_ref.shape[0]
    out[pairs - 1] = incoming(cross_ref[0], c_ref, fit, fock, drow, shift)
    for p in range(1, pairs):
        for n, offset in enumerate(offsets + (0,)):

            @pl.when(partner_ref[p] - orb == offset)
            def _():
                if n == 4:
                    rows = fock_ref[slab_ds(fit, width), :]
                    dcol = diag_col(fock_ref.at[slab_ds(fit, width), :], 0, fit, width)
                    block = self_ref[0]
                else:
                    rows = sides[n][2 * width : 3 * width, :]
                    dcol = diag_col(sides[n], 2 * width, fit, width)
                    block = block_ref[n] if n < 3 else cross_ref[0]
                out[p - 1] = own_pair(
                    block,
                    rows,
                    dcol,
                    amps_ref,
                    p,
                    fit,
                    fock,
                    drow,
                    energy_sum(energy_ref, orb, orb + offset),
                )


def gather_slabs(dst, refs, index, fit):
    width = refs[0].shape[1]
    for place, ref in enumerate(refs):
        dst[pl.ds(pl.multiple_of((place ^ fit) * width, width), width), :] = ref[index]


def first_half_body(fit_ref, orb_ref, partner_ref, up_ref, down_ref, y_ref, *refs):
    acc_ref, amps_out, mat_ref, pair_ref = refs[-4:]
    slabs = refs[:-4]
    fit = fit_ref[0]
    orb = orb_ref[0]
    near = (up_ref, down_ref, y_ref)
    for n in range(3):
        gather_slabs(mat_ref, slabs, 1 + n, fit)
        prod = mm(near[n][...], mat_ref[...], NN)
        if n == 0:
            acc_ref[...] = prod
        else:
            acc_ref[...] += prod
    gather_slabs(pair_ref, slabs, 0, fit)
    for n, offset in enumerate((REACH, -REACH)):

        @pl.when(partner_ref[0] - orb == offset)
        def _():
            acc_ref[...] += mm(near[n][...], pair_ref[...], NN)

    amps_out[...] = pair_ref[...].astype(F32).T.astype(BF16)


def last_half_body(
    fit_ref, orb_ref, partner_ref, acc_ref, own_ref, up_ref, down_ref, y_ref, low_ref, high_ref, first_ref, *refs
):
    grad_out, amps_out, sum_ref, mat_ref = refs[-4:]
    slabs = refs[:-4]
    fit = fit_ref[0]
    orb = orb_ref[0]
    half = low_ref.shape[0]
    pairs = amps_out.shape[0]
    gather_slabs(mat_ref, slabs, pairs - 1, fit)
    sum_ref[:half] = acc_ref[:half] + mm(low_ref[...], mat_ref[...], NN)
    sum_ref[half:] = acc_ref[half:] + mm(high_ref[...], mat_ref[...], NN)
    amps_out[0] = first_ref[...]
    near = (up_ref, down_ref, y_ref)
    for p in range(1, pairs):
        gather_slabs(mat_ref, slabs, p - 1, fit)
        amps_out[p] = mat_ref[...].astype(F32).T.astype(BF16)
        for n, offset in enumerate(offsets_of(orb) + (0,)):

            @pl.when(partner_ref[p] - orb == offset)
            def _():
                if n < 3:
                    sum_ref[...] += mm(near[n][...], mat_ref[...], NN)
                elif n == 3:
                    sum_ref[:half] += mm(low_ref[...], mat_ref[...], NN)
                    sum_ref[half:] += mm(high_ref[...], mat_ref[...], NN)
                else:
                    sum_ref[...] += mm(own_ref[...], mat_ref[...], NN)
                    sum_ref[...] += mm(own_ref[...], mat_ref[...], NT)

    grad_out[...] = sum_ref[...].astype(BF16)


def per_device(fit_ints, virt_fock, occ_energy, partner, old_amps):
    orbs = lax.axis_size("orb")
    fits = lax.axis_size("fit")
    orb = lax.axis_index("orb").astype(jnp.int32)
    fit = lax.axis_index("fit").astype(jnp.int32)
    orb1, fit1 = orb.reshape(1), fit.reshape(1)
    own = fit_ints[0]
    fock = virt_fock[0]
    rows, virts = own.shape
    pairs = partner.shape[0]
    width = virts // fits
    half = rows // 2
    even = orb % 2 == 0

    def over_orb(array, step):
        moves = [(i, i + step(i)) for i in range(orbs) if 0 <= i + step(i) < orbs]
        return lax.ppermute(array, "orb", moves)

    def to_up(i):
        return REACH

    def to_down(i):
        return -REACH

    def to_y(i):
        return 1 - 2 * (i % 2)

    def to_cross(i):
        return 2 * (i % 2) - 1

    def along(i):
        return REACH - 2 * REACH * (i % 2)

    def swap(array, bit):
        return lax.ppermute(array, "fit", [(i, i ^ bit) for i in range(fits)])

    def blocks(name, near):
        shape = jax.ShapeDtypeStruct((len(near), fits // 2, width, virts), F32)
        return kernel_call(blocks_body, [shape, shape], [fit1], [own] + near, name)

    def reduce_slabs(kept, sent):
        total = kept + swap(sent, 1)
        bit = 2
        while bit < fits:
            span = total.shape[1] // 2
            evens, odds = total[:, 0::2], total[:, 1::2]
            total = evens + swap(odds.astype(WIRE), bit).astype(F32)
            bit *= 2
        return total[:, 0]

    def all_slabs(slab):
        parts = {0: slab}
        bit = fits // 2
        while bit >= 1:
            for place in sorted(parts):
                parts[place ^ bit] = swap(parts[place], bit)
            bit //= 2
        return [parts[place] for place in range(fits)]

    from_up = over_orb(own, to_down)
    from_down = over_orb(own, to_up)
    from_y = over_orb(own, to_y)
    side_shape = jax.ShapeDtypeStruct((3 * width + COUNT_ROWS, virts), BF16)
    sides = kernel_call(
        side_body, [side_shape] * 4, [fit1, orb1, partner], [fock, old_amps], "side"
    )
    side_up = over_orb(sides[1], to_down)
    side_down = over_orb(sides[0], to_up)
    side_y = over_orb(sides[2], to_y)
    self_block = reduce_slabs(*blocks("self_block", [own]))

    low = over_orb(jnp.where(even, from_up[:half], from_down[:half]), to_y)
    high = over_orb(from_y[half:], along)
    side_c = over_orb(sides[3], to_cross)

    near_block = reduce_slabs(*blocks("near_blocks", [from_up, from_down, from_y]))
    early = kernel_call(
        early_body,
        jax.ShapeDtypeStruct((4, width, virts), BF16),
        [fit1, orb1, partner, occ_energy],
        [near_block, side_up, side_down, side_y, fock, old_amps],
        "early_amps",
    )
    early_slabs = all_slabs(early)

    shape = jax.ShapeDtypeStruct((1, fits // 2, width, virts), F32)
    cross_block = reduce_slabs(
        *kernel_call(split_body, [shape, shape], [fit1], [own, low, high], "cross_block")
    )
    late = kernel_call(
        late_body,
        jax.ShapeDtypeStruct((pairs, width, virts), BF16),
        [fit1, orb1, partner, occ_energy],
        [near_block, self_block, cross_block, side_up, side_down, side_y, side_c, fock, old_amps],
        "late_amps",
    )
    late_slabs = all_slabs(late)

    square = pltpu.VMEM((virts, virts), BF16)
    acc, first_amps = kernel_call(
        first_half_body,
        [jax.ShapeDtypeStruct((rows, virts), F32), jax.ShapeDtypeStruct((virts, virts), BF16)],
        [fit1, orb1, partner],
        [from_up, from_down, from_y] + early_slabs,
        "first_products",
        [square, square],
    )
    grad, new_amps = kernel_call(
        last_half_body,
        [jax.ShapeDtypeStruct((rows, virts), BF16), jax.ShapeDtypeStruct(old_amps.shape, BF16)],
        [fit1, orb1, partner],
        [acc, own, from_up, from_down, from_y, low, high, first_amps] + late_slabs,
        "last_products",
        [pltpu.VMEM((rows, virts), F32), square],
    )
    return new_amps, grad[None]


def solution(mesh):
    placed = (P("orb", "fit", None), P("orb", None, None), P(), P("orb"), P("orb", None, None))
    return jax.shard_map(
        per_device,
        mesh=mesh,
        in_specs=placed,
        out_specs=(P("orb", None, None), P("orb", "fit", None)),
        check_vma=False,
    )
```

```python
import jax
import jax.numpy as jnp
from jax import lax
from jax.experimental import pallas as pl
from jax.experimental.pallas import tpu as pltpu
from jax.sharding import PartitionSpec as P


REACH = 2
F32 = jnp.float32
BF16 = jnp.bfloat16
WIRE = jnp.float16
COUNT_ROWS = 16

SMEM = pl.BlockSpec(memory_space=pltpu.SMEM)
VMEM = pl.BlockSpec(memory_space=pltpu.VMEM)

NN = (((1,), (0,)), ((), ()))
NT = (((1,), (1,)), ((), ()))
TN = (((0,), (0,)), ((), ()))


def mm(a, b, dims):
    return lax.dot_general(a, b, dims, preferred_element_type=F32)


def cost(arrays):
    moved = sum(a.size * a.dtype.itemsize for a in arrays)
    return pl.CostEstimate(flops=200 * moved, transcendentals=0, bytes_accessed=moved)


def kernel_call(body, outs, scalars, arrays, scratch=(), grant=12):
    single = not isinstance(outs, (list, tuple))
    shapes = [outs] if single else list(outs)
    return pl.pallas_call(
        body,
        out_shape=shapes[0] if single else shapes,
        in_specs=[SMEM] * len(scalars) + [VMEM] * len(arrays),
        out_specs=VMEM if single else [VMEM] * len(shapes),
        scratch_shapes=scratch,
        cost_estimate=cost(list(arrays) + shapes),
        compiler_params=pltpu.CompilerParams(vmem_limit_bytes=grant << 20),
    )(*scalars, *arrays)


def offsets_of(orb):
    to_y = 1 - 2 * (orb % 2)
    return (REACH, -REACH, to_y, -to_y)


def slab_ds(fit, width):
    return pl.ds(pl.multiple_of(fit * width, width), width)


def side_body(partner_ref, fock_ref, amps_ref, *outs):
    width = (outs[0].shape[0] - COUNT_ROWS) // 3
    rows = slab_ds(lax.axis_index("fit"), width)
    fock_rows = fock_ref[rows, :]
    orb = lax.axis_index("orb")
    pairs = amps_ref.shape[0]
    amp_rows = [amps_ref[p, rows, :].astype(F32) for p in range(pairs)]
    prods = [mm(fock_rows, amps_ref[p], NN) for p in range(pairs)]
    for out, offset in zip(outs, offsets_of(orb)):
        amp_sum = jnp.zeros_like(amp_rows[0])
        prod_sum = jnp.zeros_like(amp_rows[0])
        count = jnp.float32(0)
        for p in range(pairs):
            hit = (partner_ref[p] - orb == offset).astype(F32)
            amp_sum = amp_sum + hit * amp_rows[p]
            prod_sum = prod_sum + hit * prods[p]
            count = count + hit
        out[:width, :] = amp_sum.astype(BF16)
        out[width : 2 * width, :] = prod_sum.astype(BF16)
        out[2 * width : 3 * width, :] = fock_rows
        out[3 * width :, :] = jnp.full((COUNT_ROWS, fock_rows.shape[1]), count, F32).astype(BF16)


def pick_body(up_ref, down_ref, y_ref, low_ref, high_ref):
    half = low_ref.shape[0]
    even = lax.axis_index("orb") % 2 == 0

    @pl.when(even)
    def _():
        low_ref[...] = up_ref[:half]

    @pl.when(jnp.logical_not(even))
    def _():
        low_ref[...] = down_ref[:half]

    high_ref[...] = y_ref[half:]


def place_slabs(prod_ref, keep, send, n, fit):
    width = keep.shape[2]
    for place in range(2 * keep.shape[0]):
        dst = send if place % 2 else keep
        dst[place // 2, n] = prod_ref[slab_ds(place ^ fit, width), :]


def blocks_body(own_ref, *refs):
    near, (keep, send, prod_ref) = refs[:-3], refs[-3:]
    own = own_ref[...]
    for n, ref in enumerate(near):
        prod_ref[...] = mm(ref[...], own, TN)
        place_slabs(prod_ref, keep, send, n, lax.axis_index("fit"))


def split_body(own_ref, low_ref, high_ref, keep, send, prod_ref):
    half = low_ref.shape[0]
    prod_ref[...] = mm(low_ref[...], own_ref[:half], TN) + mm(high_ref[...], own_ref[half:], TN)
    place_slabs(prod_ref, keep, send, 0, lax.axis_index("fit"))


def diag_row(fock):
    size = fock.shape[0]
    eye = lax.broadcasted_iota(jnp.int32, (size, size), 0) == lax.broadcasted_iota(
        jnp.int32, (size, size), 1
    )
    return jnp.sum(jnp.where(eye, fock.astype(F32), 0.0), axis=0, keepdims=True)


def diag_col(fock_rows_ref, start, fit, width):
    block = fock_rows_ref[start : start + width, slab_ds(fit, width)].astype(F32)
    eye = lax.broadcasted_iota(jnp.int32, (width, width), 0) == lax.broadcasted_iota(
        jnp.int32, (width, width), 1
    )
    return jnp.sum(jnp.where(eye, block, 0.0), axis=1, keepdims=True)


def energy_sum(energy_ref, orb, other):
    top = energy_ref.shape[0] - 1
    return energy_ref[orb] + energy_ref[jnp.clip(other, 0, top)]


def incoming(block, side_ref, fit, fock, drow, shift):
    width = block.shape[0]
    amps = side_ref[:width, :]
    wide = amps.astype(F32)
    count = side_ref[3 * width : 3 * width + 1, :].astype(F32)
    residual = count * block + side_ref[width : 2 * width, :].astype(F32)
    residual = residual + mm(amps, fock, NN) - shift * wide
    denominator = diag_col(side_ref, 2 * width, fit, width) + drow - shift
    return (wide - residual / denominator).astype(BF16)


def own_pair(block, fock_rows, dcol, amps, turned, base, drow, shift):
    residual = block + base + mm(fock_rows, amps, NT) - shift * turned
    return (turned - residual / (dcol + drow - shift)).astype(BF16)


def turn_body(fock_ref, amps_ref, turned_ref, diag_ref):
    width = turned_ref.shape[1]
    for p in range(amps_ref.shape[0]):
        turned_ref[p] = amps_ref[p, :, slab_ds(lax.axis_index("fit"), width)].astype(F32).T
    diag_ref[...] = jnp.broadcast_to(diag_row(fock_ref[...]), diag_ref.shape)


def base_body(fock_ref, turned_ref, base_ref):
    for p in range(turned_ref.shape[0]):
        base_ref[p] = mm(turned_ref[p].astype(BF16), fock_ref[...], NN)


def early_body(
    partner_ref,
    energy_ref,
    block_ref,
    up_ref,
    down_ref,
    y_ref,
    turned_ref,
    base_ref,
    diag_ref,
    fock_ref,
    amps_ref,
    out,
):
    fit = lax.axis_index("fit")
    orb = lax.axis_index("orb")
    fock = fock_ref[...]
    drow = diag_ref[:1, :]
    width = out.shape[1]
    sides = (up_ref, down_ref, y_ref)
    for n, offset in enumerate(offsets_of(orb)[:3]):
        shift = energy_sum(energy_ref, orb, orb + offset)
        out[1 + n] = incoming(block_ref[n], sides[n], fit, fock, drow, shift)
    for n, offset in enumerate((REACH, -REACH)):

        @pl.when(partner_ref[0] - orb == offset)
        def _():
            side = sides[n]
            out[0] = own_pair(
                block_ref[n],
                side[2 * width : 3 * width, :],
                diag_col(side, 2 * width, fit, width),
                amps_ref[0],
                turned_ref[0],
                base_ref[0],
                drow,
                energy_sum(energy_ref, orb, orb + offset),
            )


def late_body(
    partner_ref,
    energy_ref,
    block_ref,
    self_ref,
    cross_ref,
    up_ref,
    down_ref,
    y_ref,
    c_ref,
    turned_ref,
    base_ref,
    diag_ref,
    fock_ref,
    amps_ref,
    out,
):
    fit = lax.axis_index("fit")
    orb = lax.axis_index("orb")
    fock = fock_ref[...]
    drow = diag_ref[:1, :]
    width = out.shape[1]
    sides = (up_ref, down_ref, y_ref, c_ref)
    offsets = offsets_of(orb)
    shift = energy_sum(energy_ref, orb, orb + offsets[3])
    pairs = amps_ref.shape[0]
    out[pairs - 1] = incoming(cross_ref[0], c_ref, fit, fock, drow, shift)
    for p in range(1, pairs):
        for n, offset in enumerate(offsets + (0,)):

            @pl.when(partner_ref[p] - orb == offset)
            def _():
                if n == 4:
                    rows = fock_ref[slab_ds(fit, width), :]
                    dcol = diag_col(fock_ref.at[slab_ds(fit, width), :], 0, fit, width)
                    block = self_ref[0]
                else:
                    rows = sides[n][2 * width : 3 * width, :]
                    dcol = diag_col(sides[n], 2 * width, fit, width)
                    block = block_ref[n] if n < 3 else cross_ref[0]
                out[p - 1] = own_pair(
                    block,
                    rows,
                    dcol,
                    amps_ref[p],
                    turned_ref[p],
                    base_ref[p],
                    drow,
                    energy_sum(energy_ref, orb, orb + offset),
                )


def gather_slabs(dst, refs, index, fit):
    width = refs[0].shape[1]
    for place, ref in enumerate(refs):
        dst[pl.ds(pl.multiple_of((place ^ fit) * width, width), width), :] = ref[index]


def first_half_body(partner_ref, up_ref, down_ref, y_ref, *refs):
    acc_ref, amps_out, mat_ref, pair_ref = refs[-4:]
    slabs = refs[:-4]
    fit = lax.axis_index("fit")
    orb = lax.axis_index("orb")
    gather_slabs(pair_ref, slabs, 0, fit)
    pair = pair_ref[...].astype(F32)
    amps_out[...] = pair.T.astype(BF16)
    near = (up_ref, down_ref, y_ref)
    total = None
    for n, offset in enumerate(offsets_of(orb)[:3]):
        gather_slabs(mat_ref, slabs, 1 + n, fit)
        mat = mat_ref[...]
        if n < 2:
            hit = (partner_ref[0] - orb == offset).astype(F32)
            mat = (mat.astype(F32) + hit * pair).astype(BF16)
        prod = mm(near[n][...], mat, NN)
        total = prod if total is None else total + prod
    acc_ref[...] = total


def last_half_body(
    partner_ref, acc_ref, own_ref, up_ref, down_ref, y_ref, low_ref, high_ref, first_ref, *refs
):
    grad_out, amps_out, sum_ref, mat_ref = refs[-4:]
    slabs = refs[:-4]
    fit = lax.axis_index("fit")
    orb = lax.axis_index("orb")
    half = low_ref.shape[0]
    pairs = amps_out.shape[0]
    gather_slabs(mat_ref, slabs, pairs - 1, fit)
    sum_ref[:half] = acc_ref[:half] + mm(low_ref[...], mat_ref[...], NN)
    sum_ref[half:] = acc_ref[half:] + mm(high_ref[...], mat_ref[...], NN)
    amps_out[0] = first_ref[...]
    near = (up_ref, down_ref, y_ref)
    for p in range(1, pairs):
        gather_slabs(mat_ref, slabs, p - 1, fit)
        amps_out[p] = mat_ref[...].astype(F32).T.astype(BF16)
        for n, offset in enumerate(offsets_of(orb) + (0,)):

            @pl.when(partner_ref[p] - orb == offset)
            def _():
                if n < 3:
                    sum_ref[...] += mm(near[n][...], mat_ref[...], NN)
                elif n == 3:
                    sum_ref[:half] += mm(low_ref[...], mat_ref[...], NN)
                    sum_ref[half:] += mm(high_ref[...], mat_ref[...], NN)
                else:
                    own = own_ref[...]
                    sum_ref[...] += mm(own, mat_ref[...], NN) + mm(own, mat_ref[...], NT)

    grad_out[...] = sum_ref[...].astype(BF16)


def per_device(fit_ints, virt_fock, occ_energy, partner, old_amps):
    orbs = lax.axis_size("orb")
    fits = lax.axis_size("fit")
    own = fit_ints[0]
    fock = virt_fock[0]
    rows, virts = own.shape
    pairs = partner.shape[0]
    width = virts // fits
    half = rows // 2

    def over_orb(array, step):
        moves = [(i, i + step(i)) for i in range(orbs) if 0 <= i + step(i) < orbs]
        return lax.ppermute(array, "orb", moves)

    def to_up(i):
        return REACH

    def to_down(i):
        return -REACH

    def to_y(i):
        return 1 - 2 * (i % 2)

    def to_cross(i):
        return 2 * (i % 2) - 1

    def along(i):
        return REACH - 2 * REACH * (i % 2)

    def swap(array, bit):
        return lax.ppermute(array, "fit", [(i, i ^ bit) for i in range(fits)])

    def product_shapes(count):
        shape = jax.ShapeDtypeStruct((fits // 2, count, width, virts), F32)
        return [shape, shape]

    square = pltpu.VMEM((virts, virts), BF16)
    wide = pltpu.VMEM((virts, virts), F32)

    def reduce_slabs(kept, sent):
        total = kept + swap(sent, 1)
        bit = 2
        while bit < fits:
            evens, odds = total[0::2], total[1::2]
            total = evens + swap(odds.astype(WIRE), bit).astype(F32)
            bit *= 2
        return total[0]

    def all_slabs(slab):
        parts = {0: slab}
        bit = fits // 2
        while bit >= 1:
            for place in sorted(parts):
                parts[place ^ bit] = swap(parts[place], bit)
            bit //= 2
        return [parts[place] for place in range(fits)]

    from_up = over_orb(own, to_down)
    from_down = over_orb(own, to_up)
    from_y = over_orb(own, to_y)
    side_shape = jax.ShapeDtypeStruct((3 * width + COUNT_ROWS, virts), BF16)
    sides = kernel_call(side_body, [side_shape] * 4, [partner], [fock, old_amps])
    side_up = over_orb(sides[1], to_down)
    side_down = over_orb(sides[0], to_up)
    side_y = over_orb(sides[2], to_y)
    self_block = reduce_slabs(*kernel_call(blocks_body, product_shapes(1), [], [own, own], [wide]))

    slab_pairs = jax.ShapeDtypeStruct((pairs, width, virts), F32)
    turned, diag = kernel_call(
        turn_body, [slab_pairs, jax.ShapeDtypeStruct((8, virts), F32)], [], [fock, old_amps]
    )
    base = kernel_call(base_body, slab_pairs, [], [fock, turned])

    part = jax.ShapeDtypeStruct((half, virts), BF16)
    to_low, to_high = kernel_call(pick_body, [part, part], [], [from_up, from_down, from_y])
    low = over_orb(to_low, to_y)
    high = over_orb(to_high, along)
    side_c = over_orb(sides[3], to_cross)

    near_block = reduce_slabs(
        *kernel_call(blocks_body, product_shapes(3), [], [own, from_up, from_down, from_y], [wide]),
    )
    early = kernel_call(
        early_body,
        jax.ShapeDtypeStruct((4, width, virts), BF16),
        [partner, occ_energy],
        [near_block, side_up, side_down, side_y, turned, base, diag, fock, old_amps],
    )
    early_slabs = all_slabs(early)

    cross_block = reduce_slabs(
        *kernel_call(split_body, product_shapes(1), [], [own, low, high], [wide]),
    )
    late = kernel_call(
        late_body,
        jax.ShapeDtypeStruct((pairs, width, virts), BF16),
        [partner, occ_energy],
        [near_block, self_block, cross_block, side_up, side_down, side_y, side_c]
        + [turned, base, diag, fock, old_amps],
    )
    late_slabs = all_slabs(late)

    acc, first_amps = kernel_call(
        first_half_body,
        [jax.ShapeDtypeStruct((rows, virts), F32), jax.ShapeDtypeStruct((virts, virts), BF16)],
        [partner],
        [from_up, from_down, from_y] + early_slabs,
        [square, square],
    )
    grad, new_amps = kernel_call(
        last_half_body,
        [jax.ShapeDtypeStruct((rows, virts), BF16), jax.ShapeDtypeStruct(old_amps.shape, BF16)],
        [partner],
        [acc, own, from_up, from_down, from_y, low, high, first_amps] + late_slabs,
        [pltpu.VMEM((rows, virts), F32), square],
    )
    return new_amps, grad[None]


def solution(mesh):
    placed = (P("orb", "fit", None), P("orb", None, None), P(), P("orb"), P("orb", None, None))

    return jax.shard_map(
        per_device,
        mesh=mesh,
        in_specs=placed,
        out_specs=(P("orb", None, None), P("orb", "fit", None)),
        check_vma=False,
    )
```

```python
import jax
import jax.numpy as jnp
from jax import lax
from jax.experimental import pallas as pl
from jax.experimental.pallas import tpu as pltpu
from jax.sharding import PartitionSpec as P


REACH = 2
F32 = jnp.float32
BF16 = jnp.bfloat16
WIRE = jnp.float16
COUNT_ROWS = 16

SMEM = pl.BlockSpec(memory_space=pltpu.SMEM)
VMEM = pl.BlockSpec(memory_space=pltpu.VMEM)

NN = (((1,), (0,)), ((), ()))
NT = (((1,), (1,)), ((), ()))
TN = (((0,), (0,)), ((), ()))


def mm(a, b, dims):
    return lax.dot_general(a, b, dims, preferred_element_type=F32)


def cost(arrays):
    moved = sum(a.size * a.dtype.itemsize for a in arrays)
    return pl.CostEstimate(flops=200 * moved, transcendentals=0, bytes_accessed=moved)


def kernel_call(body, outs, scalars, arrays, scratch=(), grant=12):
    single = not isinstance(outs, (list, tuple))
    shapes = [outs] if single else list(outs)
    return pl.pallas_call(
        body,
        out_shape=shapes[0] if single else shapes,
        in_specs=[SMEM] * len(scalars) + [VMEM] * len(arrays),
        out_specs=VMEM if single else [VMEM] * len(shapes),
        scratch_shapes=scratch,
        cost_estimate=cost(list(arrays) + shapes),
        compiler_params=pltpu.CompilerParams(vmem_limit_bytes=grant << 20),
    )(*scalars, *arrays)


def offsets_of(orb):
    to_y = 1 - 2 * (orb % 2)
    return (REACH, -REACH, to_y, -to_y)


def slab_ds(fit, width):
    return pl.ds(pl.multiple_of(fit * width, width), width)


def side_body(partner_ref, fock_ref, amps_ref, *outs):
    width = (outs[0].shape[0] - COUNT_ROWS) // 3
    rows = slab_ds(lax.axis_index("fit"), width)
    fock_rows = fock_ref[rows, :]
    orb = lax.axis_index("orb")
    pairs = amps_ref.shape[0]
    amp_rows = [amps_ref[p, rows, :].astype(F32) for p in range(pairs)]
    prods = [mm(fock_rows, amps_ref[p], NN) for p in range(pairs)]
    for out, offset in zip(outs, offsets_of(orb)):
        amp_sum = jnp.zeros_like(amp_rows[0])
        prod_sum = jnp.zeros_like(amp_rows[0])
        count = jnp.float32(0)
        for p in range(pairs):
            hit = (partner_ref[p] - orb == offset).astype(F32)
            amp_sum = amp_sum + hit * amp_rows[p]
            prod_sum = prod_sum + hit * prods[p]
            count = count + hit
        out[:width, :] = amp_sum.astype(BF16)
        out[width : 2 * width, :] = prod_sum.astype(BF16)
        out[2 * width : 3 * width, :] = fock_rows
        out[3 * width :, :] = jnp.full((COUNT_ROWS, fock_rows.shape[1]), count, F32).astype(BF16)


def pick_body(up_ref, down_ref, low_ref):
    half = low_ref.shape[0]
    even = lax.axis_index("orb") % 2 == 0

    @pl.when(even)
    def _():
        low_ref[...] = up_ref[:half]

    @pl.when(jnp.logical_not(even))
    def _():
        low_ref[...] = down_ref[:half]


def place_slabs(prod_ref, keep, send, n, fit):
    width = keep.shape[2]
    for place in range(2 * keep.shape[0]):
        dst = send if place % 2 else keep
        dst[place // 2, n] = prod_ref[slab_ds(place ^ fit, width), :]


def blocks_body(own_ref, *refs):
    near, (keep, send, prod_ref) = refs[:-3], refs[-3:]
    own = own_ref[...]
    for n, ref in enumerate(near):
        prod_ref[...] = mm(ref[...], own, TN)
        place_slabs(prod_ref, keep, send, n, lax.axis_index("fit"))


def y_body(own_ref, y_ref, keep, send, high_ref, prod_ref):
    high_ref[...] = y_ref[high_ref.shape[0] :]
    blocks_body(own_ref, y_ref, keep, send, prod_ref)


def split_body(own_ref, low_ref, high_ref, keep, send, prod_ref):
    half = low_ref.shape[0]
    prod_ref[...] = mm(low_ref[...], own_ref[:half], TN) + mm(high_ref[...], own_ref[half:], TN)
    place_slabs(prod_ref, keep, send, 0, lax.axis_index("fit"))


def diag_row(fock):
    size = fock.shape[0]
    eye = lax.broadcasted_iota(jnp.int32, (size, size), 0) == lax.broadcasted_iota(
        jnp.int32, (size, size), 1
    )
    return jnp.sum(jnp.where(eye, fock.astype(F32), 0.0), axis=0, keepdims=True)


def diag_col(fock_rows_ref, start, fit, width):
    block = fock_rows_ref[start : start + width, slab_ds(fit, width)].astype(F32)
    eye = lax.broadcasted_iota(jnp.int32, (width, width), 0) == lax.broadcasted_iota(
        jnp.int32, (width, width), 1
    )
    return jnp.sum(jnp.where(eye, block, 0.0), axis=1, keepdims=True)


def energy_sum(energy_ref, orb, other):
    top = energy_ref.shape[0] - 1
    return energy_ref[orb] + energy_ref[jnp.clip(other, 0, top)]


def incoming(block, side_ref, fit, fock, drow, shift):
    width = block.shape[0]
    amps = side_ref[:width, :]
    wide = amps.astype(F32)
    count = side_ref[3 * width : 3 * width + 1, :].astype(F32)
    residual = count * block + side_ref[width : 2 * width, :].astype(F32)
    residual = residual + mm(amps, fock, NN) - shift * wide
    denominator = diag_col(side_ref, 2 * width, fit, width) + drow - shift
    return (wide - residual / denominator).astype(BF16)


def own_pair(block, fock_rows, dcol, amps, turned, base, drow, shift):
    residual = block + base + mm(fock_rows, amps, NT) - shift * turned
    return (turned - residual / (dcol + drow - shift)).astype(BF16)


def turn_body(fock_ref, amps_ref, turned_ref, diag_ref):
    width = turned_ref.shape[1]
    for p in range(amps_ref.shape[0]):
        turned_ref[p] = amps_ref[p, :, slab_ds(lax.axis_index("fit"), width)].astype(F32).T
    diag_ref[...] = jnp.broadcast_to(diag_row(fock_ref[...]), diag_ref.shape)


def base_body(fock_ref, turned_ref, base_ref):
    for p in range(turned_ref.shape[0]):
        base_ref[p] = mm(turned_ref[p].astype(BF16), fock_ref[...], NN)


def early_body(
    partner_ref,
    energy_ref,
    z_ref,
    block_ref,
    up_ref,
    down_ref,
    y_ref,
    turned_ref,
    base_ref,
    diag_ref,
    fock_ref,
    amps_ref,
    out,
):
    fit = lax.axis_index("fit")
    orb = lax.axis_index("orb")
    fock = fock_ref[...]
    drow = diag_ref[:1, :]
    width = out.shape[1]
    sides = (up_ref, down_ref, y_ref)
    for n, offset in enumerate(offsets_of(orb)[:3]):
        shift = energy_sum(energy_ref, orb, orb + offset)
        block = z_ref[n] if n < 2 else block_ref[0]
        out[1 + n] = incoming(block, sides[n], fit, fock, drow, shift)
    for n, offset in enumerate((REACH, -REACH)):

        @pl.when(partner_ref[0] - orb == offset)
        def _():
            side = sides[n]
            out[0] = own_pair(
                z_ref[n],
                side[2 * width : 3 * width, :],
                diag_col(side, 2 * width, fit, width),
                amps_ref[0],
                turned_ref[0],
                base_ref[0],
                drow,
                energy_sum(energy_ref, orb, orb + offset),
            )


def late_body(
    partner_ref,
    energy_ref,
    z_ref,
    block_ref,
    self_ref,
    cross_ref,
    up_ref,
    down_ref,
    y_ref,
    c_ref,
    turned_ref,
    base_ref,
    diag_ref,
    fock_ref,
    amps_ref,
    out,
):
    fit = lax.axis_index("fit")
    orb = lax.axis_index("orb")
    fock = fock_ref[...]
    drow = diag_ref[:1, :]
    width = out.shape[1]
    sides = (up_ref, down_ref, y_ref, c_ref)
    offsets = offsets_of(orb)
    shift = energy_sum(energy_ref, orb, orb + offsets[3])
    pairs = amps_ref.shape[0]
    out[pairs - 1] = incoming(cross_ref[0], c_ref, fit, fock, drow, shift)
    for p in range(1, pairs):
        for n, offset in enumerate(offsets + (0,)):

            @pl.when(partner_ref[p] - orb == offset)
            def _():
                if n == 4:
                    rows = fock_ref[slab_ds(fit, width), :]
                    dcol = diag_col(fock_ref.at[slab_ds(fit, width), :], 0, fit, width)
                    block = self_ref[0]
                else:
                    rows = sides[n][2 * width : 3 * width, :]
                    dcol = diag_col(sides[n], 2 * width, fit, width)
                    block = (z_ref[0], z_ref[1], block_ref[0], cross_ref[0])[n]
                out[p - 1] = own_pair(
                    block,
                    rows,
                    dcol,
                    amps_ref[p],
                    turned_ref[p],
                    base_ref[p],
                    drow,
                    energy_sum(energy_ref, orb, orb + offset),
                )


def gather_slabs(dst, refs, index, fit):
    width = refs[0].shape[1]
    for place, ref in enumerate(refs):
        dst[pl.ds(pl.multiple_of((place ^ fit) * width, width), width), :] = ref[index]


def first_half_body(partner_ref, up_ref, down_ref, y_ref, *refs):
    acc_ref, amps_out, mat_ref, pair_ref = refs[-4:]
    slabs = refs[:-4]
    fit = lax.axis_index("fit")
    orb = lax.axis_index("orb")
    gather_slabs(pair_ref, slabs, 0, fit)
    pair = pair_ref[...].astype(F32)
    amps_out[...] = pair.T.astype(BF16)
    near = (up_ref, down_ref, y_ref)
    total = None
    for n, offset in enumerate(offsets_of(orb)[:3]):
        gather_slabs(mat_ref, slabs, 1 + n, fit)
        mat = mat_ref[...]
        if n < 2:
            hit = (partner_ref[0] - orb == offset).astype(F32)
            mat = (mat.astype(F32) + hit * pair).astype(BF16)
        prod = mm(near[n][...], mat, NN)
        total = prod if total is None else total + prod
    acc_ref[...] = total


def last_half_body(
    partner_ref, acc_ref, own_ref, up_ref, down_ref, y_ref, low_ref, high_ref, first_ref, *refs
):
    grad_out, amps_out, sum_ref, mat_ref = refs[-4:]
    slabs = refs[:-4]
    fit = lax.axis_index("fit")
    orb = lax.axis_index("orb")
    half = low_ref.shape[0]
    pairs = amps_out.shape[0]
    gather_slabs(mat_ref, slabs, pairs - 1, fit)
    sum_ref[:half] = acc_ref[:half] + mm(low_ref[...], mat_ref[...], NN)
    sum_ref[half:] = acc_ref[half:] + mm(high_ref[...], mat_ref[...], NN)
    amps_out[0] = first_ref[...]
    near = (up_ref, down_ref, y_ref)
    for p in range(1, pairs):
        gather_slabs(mat_ref, slabs, p - 1, fit)
        amps_out[p] = mat_ref[...].astype(F32).T.astype(BF16)
        for n, offset in enumerate(offsets_of(orb) + (0,)):

            @pl.when(partner_ref[p] - orb == offset)
            def _():
                if n < 3:
                    sum_ref[...] += mm(near[n][...], mat_ref[...], NN)
                elif n == 3:
                    sum_ref[:half] += mm(low_ref[...], mat_ref[...], NN)
                    sum_ref[half:] += mm(high_ref[...], mat_ref[...], NN)
                else:
                    own = own_ref[...]
                    sum_ref[...] += mm(own, mat_ref[...], NN) + mm(own, mat_ref[...], NT)

    grad_out[...] = sum_ref[...].astype(BF16)


def per_device(fit_ints, virt_fock, occ_energy, partner, old_amps):
    orbs = lax.axis_size("orb")
    fits = lax.axis_size("fit")
    own = fit_ints[0]
    fock = virt_fock[0]
    rows, virts = own.shape
    pairs = partner.shape[0]
    width = virts // fits
    half = rows // 2

    def over_orb(array, step):
        moves = [(i, i + step(i)) for i in range(orbs) if 0 <= i + step(i) < orbs]
        return lax.ppermute(array, "orb", moves)

    def to_up(i):
        return REACH

    def to_down(i):
        return -REACH

    def to_y(i):
        return 1 - 2 * (i % 2)

    def to_cross(i):
        return 2 * (i % 2) - 1

    def along(i):
        return REACH - 2 * REACH * (i % 2)

    def swap(array, bit):
        return lax.ppermute(array, "fit", [(i, i ^ bit) for i in range(fits)])

    def product_shapes(count):
        shape = jax.ShapeDtypeStruct((fits // 2, count, width, virts), F32)
        return [shape, shape]

    square = pltpu.VMEM((virts, virts), BF16)
    wide = pltpu.VMEM((virts, virts), F32)

    def reduce_slabs(kept, sent):
        total = kept + swap(sent, 1)
        bit = 2
        while bit < fits:
            evens, odds = total[0::2], total[1::2]
            total = evens + swap(odds.astype(WIRE), bit).astype(F32)
            bit *= 2
        return total[0]

    def all_slabs(slab):
        parts = {0: slab}
        bit = fits // 2
        while bit >= 1:
            for place in sorted(parts):
                parts[place ^ bit] = swap(parts[place], bit)
            bit //= 2
        return [parts[place] for place in range(fits)]

    from_y = over_orb(own, to_y)
    from_up = over_orb(own, to_down)
    from_down = over_orb(own, to_up)
    side_shape = jax.ShapeDtypeStruct((3 * width + COUNT_ROWS, virts), BF16)
    sides = kernel_call(side_body, [side_shape] * 4, [partner], [fock, old_amps])
    side_y = over_orb(sides[2], to_y)
    side_up = over_orb(sides[1], to_down)
    side_down = over_orb(sides[0], to_up)
    self_block = reduce_slabs(*kernel_call(blocks_body, product_shapes(1), [], [own, own], [wide]))

    slab_pairs = jax.ShapeDtypeStruct((pairs, width, virts), F32)
    turned, diag = kernel_call(
        turn_body, [slab_pairs, jax.ShapeDtypeStruct((8, virts), F32)], [], [fock, old_amps]
    )
    base = kernel_call(base_body, slab_pairs, [], [fock, turned])

    part = jax.ShapeDtypeStruct((half, virts), BF16)
    kept, sent, to_high = kernel_call(y_body, product_shapes(1) + [part], [], [own, from_y], [wide])
    high = over_orb(to_high, along)
    y_block = reduce_slabs(kept, sent)
    to_low = kernel_call(pick_body, part, [], [from_up, from_down])
    low = over_orb(to_low, to_y)
    side_c = over_orb(sides[3], to_cross)
    z_blocks = reduce_slabs(
        *kernel_call(blocks_body, product_shapes(2), [], [own, from_up, from_down], [wide]),
    )
    early = kernel_call(
        early_body,
        jax.ShapeDtypeStruct((4, width, virts), BF16),
        [partner, occ_energy],
        [z_blocks, y_block, side_up, side_down, side_y, turned, base, diag, fock, old_amps],
    )
    early_slabs = all_slabs(early)

    cross_block = reduce_slabs(
        *kernel_call(split_body, product_shapes(1), [], [own, low, high], [wide]),
    )
    late = kernel_call(
        late_body,
        jax.ShapeDtypeStruct((pairs, width, virts), BF16),
        [partner, occ_energy],
        [z_blocks, y_block, self_block, cross_block, side_up, side_down, side_y, side_c]
        + [turned, base, diag, fock, old_amps],
    )
    late_slabs = all_slabs(late)

    acc, first_amps = kernel_call(
        first_half_body,
        [jax.ShapeDtypeStruct((rows, virts), F32), jax.ShapeDtypeStruct((virts, virts), BF16)],
        [partner],
        [from_up, from_down, from_y] + early_slabs,
        [square, square],
    )
    grad, new_amps = kernel_call(
        last_half_body,
        [jax.ShapeDtypeStruct((rows, virts), BF16), jax.ShapeDtypeStruct(old_amps.shape, BF16)],
        [partner],
        [acc, own, from_up, from_down, from_y, low, high, first_amps] + late_slabs,
        [pltpu.VMEM((rows, virts), F32), square],
    )
    return new_amps, grad[None]


def solution(mesh):
    placed = (P("orb", "fit", None), P("orb", None, None), P(), P("orb"), P("orb", None, None))

    return jax.shard_map(
        per_device,
        mesh=mesh,
        in_specs=placed,
        out_specs=(P("orb", None, None), P("orb", "fit", None)),
        check_vma=False,
    )
```

```python
import jax
import jax.numpy as jnp
from jax import lax
from jax.experimental import pallas as pl
from jax.experimental.pallas import tpu as pltpu
from jax.sharding import PartitionSpec as P


REACH = 2
F32 = jnp.float32
BF16 = jnp.bfloat16
WIRE = jnp.float16
COUNT_ROWS = 16

SMEM = pl.BlockSpec(memory_space=pltpu.SMEM)
VMEM = pl.BlockSpec(memory_space=pltpu.VMEM)

NN = (((1,), (0,)), ((), ()))
NT = (((1,), (1,)), ((), ()))
TN = (((0,), (0,)), ((), ()))


def mm(a, b, dims):
    return lax.dot_general(a, b, dims, preferred_element_type=F32)


def cost(arrays):
    moved = sum(a.size * a.dtype.itemsize for a in arrays)
    return pl.CostEstimate(flops=200 * moved, transcendentals=0, bytes_accessed=moved)


def kernel_call(body, outs, scalars, arrays, scratch=(), grant=12, out_spec=VMEM):
    single = not isinstance(outs, (list, tuple))
    shapes = [outs] if single else list(outs)
    return pl.pallas_call(
        body,
        out_shape=shapes[0] if single else shapes,
        in_specs=[SMEM] * len(scalars) + [VMEM] * len(arrays),
        out_specs=out_spec if single else [out_spec] * len(shapes),
        scratch_shapes=scratch,
        cost_estimate=cost(list(arrays) + shapes),
        compiler_params=pltpu.CompilerParams(vmem_limit_bytes=grant << 20),
    )(*scalars, *arrays)


def offsets_of(orb):
    to_y = 1 - 2 * (orb % 2)
    return (REACH, -REACH, to_y, -to_y)


def slab_ds(fit, width):
    return pl.ds(pl.multiple_of(fit * width, width), width)


def side_body(partner_ref, fock_ref, amps_ref, *outs):
    width = (outs[0].shape[0] - COUNT_ROWS) // 3
    rows = slab_ds(lax.axis_index("fit"), width)
    fock_rows = fock_ref[rows, :]
    orb = lax.axis_index("orb")
    pairs = amps_ref.shape[0]
    amp_rows = [amps_ref[p, rows, :].astype(F32) for p in range(pairs)]
    prods = [mm(fock_rows, amps_ref[p], NN) for p in range(pairs)]
    for out, offset in zip(outs, offsets_of(orb)):
        amp_sum = jnp.zeros_like(amp_rows[0])
        prod_sum = jnp.zeros_like(amp_rows[0])
        count = jnp.float32(0)
        for p in range(pairs):
            hit = (partner_ref[p] - orb == offset).astype(F32)
            amp_sum = amp_sum + hit * amp_rows[p]
            prod_sum = prod_sum + hit * prods[p]
            count = count + hit
        out[:width, :] = amp_sum.astype(BF16)
        out[width : 2 * width, :] = prod_sum.astype(BF16)
        out[2 * width : 3 * width, :] = fock_rows
        out[3 * width :, :] = jnp.full((COUNT_ROWS, fock_rows.shape[1]), count, F32).astype(BF16)


def pick_body(up_ref, down_ref, low_ref):
    half = low_ref.shape[0]
    even = lax.axis_index("orb") % 2 == 0

    @pl.when(even)
    def _():
        low_ref[...] = up_ref[:half]

    @pl.when(jnp.logical_not(even))
    def _():
        low_ref[...] = down_ref[:half]


def place_slabs(prod_ref, keep, send, n, fit):
    width = keep.shape[2]
    for place in range(2 * keep.shape[0]):
        dst = send if place % 2 else keep
        dst[place // 2, n] = prod_ref[slab_ds(place ^ fit, width), :]


def blocks_body(own_ref, *refs):
    near, (keep, send, prod_ref) = refs[:-3], refs[-3:]
    own = own_ref[...]
    for n, ref in enumerate(near):
        prod_ref[...] = mm(ref[...], own, TN)
        place_slabs(prod_ref, keep, send, n, lax.axis_index("fit"))


def y_body(own_ref, y_ref, keep, send, high_ref, prod_ref):
    high_ref[...] = y_ref[high_ref.shape[0] :]
    blocks_body(own_ref, y_ref, keep, send, prod_ref)


def split_body(own_ref, low_ref, high_ref, keep, send, prod_ref):
    half = low_ref.shape[0]
    prod_ref[...] = mm(low_ref[...], own_ref[:half], TN) + mm(high_ref[...], own_ref[half:], TN)
    place_slabs(prod_ref, keep, send, 0, lax.axis_index("fit"))


def diag_row(fock):
    size = fock.shape[0]
    eye = lax.broadcasted_iota(jnp.int32, (size, size), 0) == lax.broadcasted_iota(
        jnp.int32, (size, size), 1
    )
    return jnp.sum(jnp.where(eye, fock.astype(F32), 0.0), axis=0, keepdims=True)


def diag_col(fock_rows_ref, start, fit, width):
    block = fock_rows_ref[start : start + width, slab_ds(fit, width)].astype(F32)
    eye = lax.broadcasted_iota(jnp.int32, (width, width), 0) == lax.broadcasted_iota(
        jnp.int32, (width, width), 1
    )
    return jnp.sum(jnp.where(eye, block, 0.0), axis=1, keepdims=True)


def energy_sum(energy_ref, orb, other):
    top = energy_ref.shape[0] - 1
    return energy_ref[orb] + energy_ref[jnp.clip(other, 0, top)]


def incoming(block, side_ref, fit, fock, drow, shift):
    width = block.shape[0]
    amps = side_ref[:width, :]
    wide = amps.astype(F32)
    count = side_ref[3 * width : 3 * width + 1, :].astype(F32)
    residual = count * block + side_ref[width : 2 * width, :].astype(F32)
    residual = residual + mm(amps, fock, NN) - shift * wide
    denominator = diag_col(side_ref, 2 * width, fit, width) + drow - shift
    return (wide - residual / denominator).astype(BF16)


def own_pair(block, fock_rows, dcol, amps, turned, base, drow, shift):
    residual = block + base + mm(fock_rows, amps, NT) - shift * turned
    return (turned - residual / (dcol + drow - shift)).astype(BF16)


def turn_body(fock_ref, amps_ref, turned_ref, diag_ref):
    width = turned_ref.shape[1]
    for p in range(amps_ref.shape[0]):
        turned_ref[p] = amps_ref[p, :, slab_ds(lax.axis_index("fit"), width)].astype(F32).T
    diag_ref[...] = jnp.broadcast_to(diag_row(fock_ref[...]), diag_ref.shape)


def base_body(fock_ref, turned_ref, base_ref):
    for p in range(turned_ref.shape[0]):
        base_ref[p] = mm(turned_ref[p].astype(BF16), fock_ref[...], NN)


def y_amps_body(energy_ref, block_ref, y_ref, diag_ref, fock_ref, out):
    orb = lax.axis_index("orb")
    offset = offsets_of(orb)[2]
    shift = energy_sum(energy_ref, orb, orb + offset)
    out[0] = incoming(
        block_ref[0], y_ref, lax.axis_index("fit"), fock_ref[...], diag_ref[:1, :], shift
    )


def early_body(
    partner_ref,
    energy_ref,
    block_ref,
    up_ref,
    down_ref,
    turned_ref,
    base_ref,
    diag_ref,
    fock_ref,
    amps_ref,
    out,
):
    fit = lax.axis_index("fit")
    orb = lax.axis_index("orb")
    fock = fock_ref[...]
    drow = diag_ref[:1, :]
    width = out.shape[1]
    sides = (up_ref, down_ref)
    for n, offset in enumerate((REACH, -REACH)):
        shift = energy_sum(energy_ref, orb, orb + offset)
        out[1 + n] = incoming(block_ref[n], sides[n], fit, fock, drow, shift)

        @pl.when(partner_ref[0] - orb == offset)
        def _():
            side = sides[n]
            out[0] = own_pair(
                block_ref[n],
                side[2 * width : 3 * width, :],
                diag_col(side, 2 * width, fit, width),
                amps_ref[0],
                turned_ref[0],
                base_ref[0],
                drow,
                shift,
            )


def late_body(
    partner_ref,
    energy_ref,
    z_ref,
    block_ref,
    self_ref,
    cross_ref,
    up_ref,
    down_ref,
    y_ref,
    c_ref,
    turned_ref,
    base_ref,
    diag_ref,
    fock_ref,
    amps_ref,
    out,
):
    fit = lax.axis_index("fit")
    orb = lax.axis_index("orb")
    fock = fock_ref[...]
    drow = diag_ref[:1, :]
    width = out.shape[1]
    sides = (up_ref, down_ref, y_ref, c_ref)
    offsets = offsets_of(orb)
    shift = energy_sum(energy_ref, orb, orb + offsets[3])
    pairs = amps_ref.shape[0]
    out[pairs - 1] = incoming(cross_ref[0], c_ref, fit, fock, drow, shift)
    for p in range(1, pairs):
        for n, offset in enumerate(offsets + (0,)):

            @pl.when(partner_ref[p] - orb == offset)
            def _():
                if n == 4:
                    rows = fock_ref[slab_ds(fit, width), :]
                    dcol = diag_col(fock_ref.at[slab_ds(fit, width), :], 0, fit, width)
                    block = self_ref[0]
                else:
                    rows = sides[n][2 * width : 3 * width, :]
                    dcol = diag_col(sides[n], 2 * width, fit, width)
                    block = (z_ref[0], z_ref[1], block_ref[0], cross_ref[0])[n]
                out[p - 1] = own_pair(
                    block,
                    rows,
                    dcol,
                    amps_ref[p],
                    turned_ref[p],
                    base_ref[p],
                    drow,
                    energy_sum(energy_ref, orb, orb + offset),
                )


def gather_slabs(dst, refs, index, fit):
    width = refs[0].shape[1]
    for place, ref in enumerate(refs):
        dst[pl.ds(pl.multiple_of((place ^ fit) * width, width), width), :] = ref[index]


def first_half_body(partner_ref, up_ref, down_ref, y_ref, *refs):
    acc_ref, amps_out, mats_ref, pair_ref = refs[-4:]
    count = (len(refs) - 4) // 2
    slabs, y_slabs = refs[:count], refs[count : 2 * count]
    fit = lax.axis_index("fit")
    orb = lax.axis_index("orb")
    gather_slabs(mats_ref.at[2], y_slabs, 0, fit)
    total = mm(y_ref[...], mats_ref[2], NN)
    gather_slabs(pair_ref, slabs, 0, fit)
    pair = pair_ref[...].astype(F32)
    amps_out[...] = pair.T.astype(BF16)
    near = (up_ref, down_ref)
    for n, offset in enumerate((REACH, -REACH)):
        gather_slabs(mats_ref.at[n], slabs, 1 + n, fit)
        hit = (partner_ref[0] - orb == offset).astype(F32)
        mat = (mats_ref[n].astype(F32) + hit * pair).astype(BF16)
        total = total + mm(near[n][...], mat, NN)
    acc_ref[...] = total


def last_half_body(
    partner_ref, acc_ref, own_ref, up_ref, down_ref, y_ref, low_ref, high_ref, first_ref, *refs
):
    grad_out, amps_out, sum_ref, grad_ref, mats_ref, turned_ref, sems = refs[-7:]
    slabs = refs[:-7]
    fit = lax.axis_index("fit")
    orb = lax.axis_index("orb")
    half = low_ref.shape[0]
    pairs = amps_out.shape[0]
    copies = [pltpu.make_async_copy(first_ref, amps_out.at[0], sems.at[0])]
    copies[0].start()
    near = (up_ref, down_ref, y_ref)
    total_ref = acc_ref
    for p in range(1, pairs):
        mat_ref = mats_ref.at[p - 1]
        gather_slabs(mat_ref, slabs, p - 1, fit)
        turned_ref[p - 1] = mat_ref[...].astype(F32).T.astype(BF16)
        copy = pltpu.make_async_copy(turned_ref.at[p - 1], amps_out.at[p], sems.at[p])
        copy.start()
        copies.append(copy)
        for n, offset in enumerate(offsets_of(orb) + (0,)):

            @pl.when(partner_ref[p] - orb == offset)
            def _():
                mat = mat_ref[...]
                if n < 3:
                    sum_ref[...] = total_ref[...] + mm(near[n][...], mat, NN)
                elif n == 3:
                    sum_ref[:half] = total_ref[:half] + mm(low_ref[...], mat, NN)
                    sum_ref[half:] = total_ref[half:] + mm(high_ref[...], mat, NN)
                else:
                    own = own_ref[...]
                    sum_ref[...] = total_ref[...] + mm(own, mat, NN) + mm(own, mat, NT)

        total_ref = sum_ref
    mat_ref = mats_ref.at[pairs - 1]
    gather_slabs(mat_ref, slabs, pairs - 1, fit)
    for h, part in enumerate((low_ref, high_ref)):
        rows = slice(h * half, (h + 1) * half)
        grad_ref[rows] = (total_ref[rows] + mm(part[...], mat_ref[...], NN)).astype(BF16)
        copy = pltpu.make_async_copy(
            grad_ref.at[pl.ds(h * half, half)],
            grad_out.at[pl.ds(h * half, half)],
            sems.at[pairs + h],
        )
        copy.start()
        copies.append(copy)
    for copy in copies:
        copy.wait()


def per_device(fit_ints, virt_fock, occ_energy, partner, old_amps):
    orbs = lax.axis_size("orb")
    fits = lax.axis_size("fit")
    own = fit_ints[0]
    fock = virt_fock[0]
    rows, virts = own.shape
    pairs = partner.shape[0]
    width = virts // fits
    half = rows // 2

    def over_orb(array, step):
        moves = [(i, i + step(i)) for i in range(orbs) if 0 <= i + step(i) < orbs]
        return lax.ppermute(array, "orb", moves)

    def to_up(i):
        return REACH

    def to_down(i):
        return -REACH

    def to_y(i):
        return 1 - 2 * (i % 2)

    def to_cross(i):
        return 2 * (i % 2) - 1

    def along(i):
        return REACH - 2 * REACH * (i % 2)

    def swap(array, bit):
        return lax.ppermute(array, "fit", [(i, i ^ bit) for i in range(fits)])

    def product_shapes(count):
        shape = jax.ShapeDtypeStruct((fits // 2, count, width, virts), F32)
        return [shape, shape]

    square = pltpu.VMEM((virts, virts), BF16)
    wide = pltpu.VMEM((virts, virts), F32)

    def reduce_slabs(kept, sent):
        total = kept + swap(sent.astype(WIRE), 1).astype(F32)
        bit = 2
        while bit < fits:
            evens, odds = total[0::2], total[1::2]
            total = evens + swap(odds.astype(WIRE), bit).astype(F32)
            bit *= 2
        return total[0]

    def all_slabs(slab):
        parts = {0: slab}
        bit = fits // 2
        while bit >= 1:
            for place in sorted(parts):
                parts[place ^ bit] = swap(parts[place], bit)
            bit //= 2
        return [parts[place] for place in range(fits)]

    from_y = over_orb(own, to_y)
    from_up = over_orb(own, to_down)
    from_down = over_orb(own, to_up)
    side_shape = jax.ShapeDtypeStruct((3 * width + COUNT_ROWS, virts), BF16)
    sides = kernel_call(side_body, [side_shape] * 4, [partner], [fock, old_amps])
    side_y = over_orb(sides[2], to_y)
    side_up = over_orb(sides[1], to_down)
    side_down = over_orb(sides[0], to_up)
    self_block = reduce_slabs(*kernel_call(blocks_body, product_shapes(1), [], [own, own], [wide]))

    slab_pairs = jax.ShapeDtypeStruct((pairs, width, virts), F32)
    turned, diag = kernel_call(
        turn_body, [slab_pairs, jax.ShapeDtypeStruct((8, virts), F32)], [], [fock, old_amps]
    )
    base = kernel_call(base_body, slab_pairs, [], [fock, turned])

    part = jax.ShapeDtypeStruct((half, virts), BF16)
    kept, sent, to_high = kernel_call(y_body, product_shapes(1) + [part], [], [own, from_y], [wide])
    high = over_orb(to_high, along)
    y_block = reduce_slabs(kept, sent)
    to_low = kernel_call(pick_body, part, [], [from_up, from_down])
    low = over_orb(to_low, to_y)
    side_c = over_orb(sides[3], to_cross)
    z_blocks = reduce_slabs(
        *kernel_call(blocks_body, product_shapes(2), [], [own, from_up, from_down], [wide]),
    )
    y_amps = kernel_call(
        y_amps_body,
        jax.ShapeDtypeStruct((1, width, virts), BF16),
        [occ_energy],
        [y_block, side_y, diag, fock],
    )
    y_slabs = all_slabs(y_amps)
    early = kernel_call(
        early_body,
        jax.ShapeDtypeStruct((3, width, virts), BF16),
        [partner, occ_energy],
        [z_blocks, side_up, side_down, turned, base, diag, fock, old_amps],
    )
    early_slabs = all_slabs(early)

    cross_block = reduce_slabs(
        *kernel_call(split_body, product_shapes(1), [], [own, low, high], [wide]),
    )
    late = kernel_call(
        late_body,
        jax.ShapeDtypeStruct((pairs, width, virts), BF16),
        [partner, occ_energy],
        [z_blocks, y_block, self_block, cross_block, side_up, side_down, side_y, side_c]
        + [turned, base, diag, fock, old_amps],
    )
    late_slabs = all_slabs(late)

    acc, first_amps = kernel_call(
        first_half_body,
        [jax.ShapeDtypeStruct((rows, virts), F32), jax.ShapeDtypeStruct((virts, virts), BF16)],
        [partner],
        [from_up, from_down, from_y] + early_slabs + y_slabs,
        [pltpu.VMEM((3, virts, virts), BF16), square],
    )
    grad, new_amps = kernel_call(
        last_half_body,
        [jax.ShapeDtypeStruct((rows, virts), BF16), jax.ShapeDtypeStruct(old_amps.shape, BF16)],
        [partner],
        [acc, own, from_up, from_down, from_y, low, high, first_amps] + late_slabs,
        [
            pltpu.VMEM((rows, virts), F32),
            pltpu.VMEM((rows, virts), BF16),
            pltpu.VMEM((pairs, virts, virts), BF16),
            pltpu.VMEM((pairs - 1, virts, virts), BF16),
            pltpu.SemaphoreType.DMA((pairs + 2,)),
        ],
        out_spec=pl.BlockSpec(memory_space=pl.ANY),
    )
    return new_amps, grad[None]


def solution(mesh):
    placed = (P("orb", "fit", None), P("orb", None, None), P(), P("orb"), P("orb", None, None))

    return jax.shard_map(
        per_device,
        mesh=mesh,
        in_specs=placed,
        out_specs=(P("orb", None, None), P("orb", "fit", None)),
        check_vma=False,
    )
```
